32 devices in a mesh: mom: 4 (over x, core), tm: 8 (over z, y).
Axes of the slice: x: 2, y: 2, z: 4, core: 2. Of those that a mesh axis runs over, the one named last changes fastest.
Arguments:
- hist_less: bfloat16 [2, 64, 1024, 1024], P(None, 'mom', None, 'tm'), may hold values from -6 to 6
- hist_great: bfloat16 [2, 64, 1024, 1024], P(None, 'mom', None, 'tm'), may hold values from -6 to 6
- row_less: float32 [2, 64, 1024], P(None, 'mom', 'tm'), may hold values from -6 to 6
- row_great: float32 [2, 64, 1024], P(None, 'mom', 'tm'), may hold values from -6 to 6
- mom_table: int32 [64], replicated, may hold values from 0 to 63, each once
Outputs:
- out_less: float32 [2, 64, 1024], P(None, 'mom', 'tm')
- out_great: float32 [2, 64, 1024], P(None, 'mom', 'tm')
The draws below stay inside these ranges and needn't reach their ends.
Inputs may be any that keep to these rules, and one draw needn't show every extreme that they name: `mom_table`: each slot holds a different lattice momentum.
All inputs are finite; a program needn't handle non-finite values.
Results may differ from the reference program's by a relative error of at most 0.004.
Values may be sent and summed in bfloat16 or wider, within the bound.
No kernel may reach another device: no remote copies, remote signals or barrier semaphores. Data moves between devices by JAX's collectives and lax.ppermute only.
A program may use at most 128 MiB of HBM per device.

```python
import math
import jax
import jax.numpy as jnp
from jax import lax

LSIDE = 8
K = 64
TIMES = 1024
NEW = 2
PASS = 2


def shard_levels(rng, dims, cuts, least, high):
    def one(position, shards_of):
        heights = jax.random.uniform(jax.random.fold_in(jax.random.fold_in(rng, 6), position), (shards_of,), jnp.float32, least / len(cuts), high / len(cuts))
        return jnp.repeat(jnp.exp(heights), dims[position] // shards_of).reshape((-1,) + (1,) * (len(dims) - position - 1))

    factor_of = one(*cuts[0])
    for cut in cuts[1:]:
        factor_of = factor_of * one(*cut)
    return factor_of


def centred(own_key, extent, deviation, most, pieces=(), kind=jnp.bfloat16):
    level = shard_levels(own_key, extent, pieces, -0.22, 0.18) if pieces else 1.0
    entries = jax.random.normal(own_key, extent, jnp.float32) * deviation * level
    return jnp.minimum(jnp.maximum(entries, -most), most).astype(kind)


def setup_inputs(seed: int = 0) -> dict:
    key_of = jax.random.split(jax.random.key(seed), 6)
    hist_less = centred(key_of[0], (2, K, TIMES, TIMES), 1.0, 6.0, ((1, 4), (3, 8)))
    hist_great = centred(key_of[1], (2, K, TIMES, TIMES), 1.0, 6.0, ((1, 4), (3, 8)))
    row_less = centred(key_of[2], (2, K, TIMES), 1.0, 6.0, ((1, 4), (2, 8)), jnp.float32)
    row_great = centred(key_of[3], (2, K, TIMES), 1.0, 6.0, ((1, 4), (2, 8)), jnp.float32)
    mom_table = jax.random.permutation(key_of[4], K).astype(jnp.int32)
    return dict(hist_less=hist_less, hist_great=hist_great, row_less=row_less, row_great=row_great, mom_table=mom_table)


coupling = 1.0
time_step = 0.08


def tables(mom_table, side):
    mom_x = (mom_table // side).astype(jnp.float32)
    mom_y = (mom_table % side).astype(jnp.float32)
    site_index = jnp.arange(side * side, dtype=jnp.int32)
    site_x = (site_index // side).astype(jnp.float32)
    site_y = (site_index % side).astype(jnp.float32)
    factor = 2.0 * math.pi / side
    phase_grid = factor * (site_x[:, None] * mom_x[None, :] + site_y[:, None] * mom_y[None, :])
    energy = -2.0 * (jnp.cos(factor * mom_x) + jnp.cos(factor * mom_y))
    return jnp.cos(phase_grid), jnp.sin(phase_grid), energy


def self_energy(current, cos_tab, sin_tab):
    count = current.shape[2]
    high = lax.Precision.HIGHEST

    def forward(table, block):
        return jnp.einsum('rk,akp->arp', table, block, precision=high)

    def backward(table, block):
        return jnp.einsum('rk,arp->akp', table, block, precision=high)

    real_part, imag_part = current[0], current[1]
    g_real = (forward(cos_tab, real_part) - forward(sin_tab, imag_part)) / count
    g_imag = (forward(sin_tab, real_part) + forward(cos_tab, imag_part)) / count
    less_real, less_imag = g_real[0], g_imag[0]
    great_real, great_imag = g_real[1], g_imag[1]
    scale = -coupling * coupling
    less_sq_real = less_real * less_real - less_imag * less_imag
    less_sq_imag = 2.0 * less_real * less_imag
    great_sq_real = great_real * great_real - great_imag * great_imag
    great_sq_imag = 2.0 * great_real * great_imag
    sig_less_real = scale * (less_sq_real * great_real + less_sq_imag * great_imag)
    sig_less_imag = scale * (less_sq_imag * great_real - less_sq_real * great_imag)
    sig_great_real = scale * (great_sq_real * less_real + great_sq_imag * less_imag)
    sig_great_imag = scale * (great_sq_imag * less_real - great_sq_real * less_imag)
    site_real = jnp.stack([sig_less_real, sig_great_real])
    site_imag = jnp.stack([sig_less_imag, sig_great_imag])
    out_real = backward(cos_tab, site_real) + backward(sin_tab, site_imag)
    out_imag = backward(cos_tab, site_imag) - backward(sin_tab, site_real)
    return jnp.stack([out_real, out_imag])


def exact_sum(vector, matrix):
    prods = jnp.einsum('cks,dksu->cdku', vector.astype(jnp.float32), matrix.astype(jnp.float32),
                       precision=lax.Precision.HIGHEST)
    return jnp.stack([prods[0, 0] - prods[1, 1], prods[0, 1] + prods[1, 0]])


def contract(sigma, h_less, h_great, mask, summer):
    below = mask[None, None]
    swapped = jnp.where(below, h_great, h_less)
    kept = jnp.where(below, h_less, h_great)
    sig_less = sigma[:, 0]
    sig_great = sigma[:, 1]
    lesser = summer(sig_great, h_less) - summer(sig_less, swapped)
    greater = summer(sig_great, kept) - summer(sig_less, h_great)
    return jnp.stack([lesser, greater], axis=1)


def integral(sigma, hist_less, hist_great):
    total = hist_less.shape[2]
    index_all = jnp.arange(total, dtype=jnp.int32)
    mask = index_all[:, None] < index_all[None, :]

    def one_mom(slot):
        part_sig = lax.dynamic_slice_in_dim(sigma, slot, 1, 2)
        part_less = lax.dynamic_slice_in_dim(hist_less, slot, 1, 1)
        part_great = lax.dynamic_slice_in_dim(hist_great, slot, 1, 1)
        return contract(part_sig, part_less, part_great, mask, exact_sum)

    out_all = lax.map(one_mom, jnp.arange(sigma.shape[2], dtype=jnp.int32))
    return jnp.moveaxis(out_all[:, :, :, 0, :], 0, 2)


def rotate(values, phases):
    cos_part = jnp.cos(phases)[None, :, None]
    sin_part = jnp.sin(phases)[None, :, None]
    real_part = cos_part * values[0] + sin_part * values[1]
    imag_part = cos_part * values[1] - sin_part * values[0]
    return jnp.stack([real_part, imag_part])


def turn(values):
    return jnp.stack([values[1], -values[0]])


def propagate(current, energy, evaluate):
    memory, density = evaluate(current)
    for index_new in range(NEW):
        phases = (energy + coupling * density) * time_step
        trial = rotate(current + time_step * turn(memory), phases)
        for index_pass in range(PASS):
            memory_new, density_new = evaluate(trial)
            phases = (energy + coupling * 0.5 * (density + density_new)) * time_step
            trial = rotate(current + 0.5 * time_step * turn(memory), phases) + 0.5 * time_step * turn(memory_new)
        current = trial
        if index_new + 1 < NEW:
            memory, density = evaluate(current)
    return current


def reference(hist_less, hist_great, row_less, row_great, mom_table):
    cos_tab, sin_tab, energy = tables(mom_table, LSIDE)

    def evaluate(current):
        last_col = current[:, 0, :, -1]
        density = jnp.sum(last_col * last_col) / K
        sigma = self_energy(current, cos_tab, sin_tab).astype(jnp.bfloat16)
        return integral(sigma, hist_less, hist_great), density

    current = jnp.stack([row_less, row_great], axis=1)
    final = propagate(current, energy, evaluate)
    return final[:, 0], final[:, 1]
```

```python
import math

import jax
import jax.numpy as jnp
from jax import lax
from jax.experimental import pallas as pl
from jax.experimental.pallas import tpu as pltpu
from jax.sharding import PartitionSpec as P

LSIDE = 8
NEW = 2
PASS = 2

coupling = 1.0
time_step = 0.08

F32 = jnp.float32
BF16 = jnp.bfloat16
LANES = 128
EXTRA = 16
MIB = 1 << 20


def split_two(values):
    high = values.astype(BF16)
    return high, (values - high.astype(F32)).astype(BF16)


def three_products(table, block):
    high, low = split_two(block)
    return jnp.dot(table, jnp.concatenate([high, low, high], axis=0), preferred_element_type=F32)


def prepare(hist_less, hist_great, mom_table, mom_count):
    _, moms, rows, width = hist_less.shape
    count = moms * mom_count
    sites = LSIDE * LSIDE
    factor = 2.0 * math.pi / LSIDE

    def body(less_ref, great_ref, mom_ref, out_ref, forward_ref, backward_ref, energy_ref, table_ref, sems):
        tm_pos = lax.axis_index("tm")
        mom_pos = lax.axis_index("mom")

        def copies(mom):
            made = []
            for which, ref in enumerate((less_ref, great_ref)):
                for part in range(2):
                    col = (2 * which + part) * width
                    made.append(
                        pltpu.make_async_copy(
                            ref.at[part, mom],
                            out_ref.at[mom, pl.ds(0, rows), pl.ds(col, width)],
                            sems.at[mom, 2 * which + part],
                        )
                    )
            return made

        for mom in range(moms):
            for one in copies(mom):
                one.start()

        moms_row = mom_ref[...]
        own_index = lax.broadcasted_iota(jnp.int32, (moms, count), 0) + mom_pos * moms
        own_lane = lax.broadcasted_iota(jnp.int32, (moms, count), 1)
        moms_own = jnp.sum(jnp.where(own_index == own_lane, moms_row.astype(F32), 0.0), axis=1, keepdims=True)
        moms_own = moms_own.astype(jnp.int32)

        def split_index(index):
            return lax.div(index, LSIDE).astype(F32), lax.rem(index, LSIDE).astype(F32)

        def store_split(out, table):
            high = table.astype(BF16)
            low = (table - high.astype(F32)).astype(BF16)
            depth = table.shape[1]
            out[:, :depth] = high
            out[:, depth : 2 * depth] = high
            out[:, 2 * depth :] = low

        site_x, site_y = split_index(lax.broadcasted_iota(jnp.int32, (sites, count), 0))
        mom_x, mom_y = split_index(jnp.broadcast_to(moms_row, (sites, count)))
        phase = factor * (site_x * mom_x + site_y * mom_y)
        cos_tab, sin_tab = jnp.cos(phase), jnp.sin(phase)
        table_ref[:sites, :count] = cos_tab
        table_ref[:sites, count:] = -sin_tab
        table_ref[sites:, :count] = sin_tab
        table_ref[sites:, count:] = cos_tab
        store_split(forward_ref, table_ref[...])
        site_x, site_y = split_index(lax.broadcasted_iota(jnp.int32, (moms, sites), 1))
        mom_x, mom_y = split_index(jnp.broadcast_to(moms_own, (moms, sites)))
        phase = factor * (site_x * mom_x + site_y * mom_y)
        cos_tab, sin_tab = jnp.cos(phase), jnp.sin(phase)
        table_ref[:moms, :sites] = cos_tab
        table_ref[:moms, sites:] = sin_tab
        table_ref[moms : 2 * moms, :sites] = -sin_tab
        table_ref[moms : 2 * moms, sites:] = cos_tab
        store_split(backward_ref, table_ref[: 2 * moms, :])
        mom_x, mom_y = split_index(jnp.broadcast_to(moms_own, (moms, width)))
        energy_ref[...] = -2.0 * (jnp.cos(factor * mom_x) + jnp.cos(factor * mom_y))

        row_index = lax.broadcasted_iota(jnp.int32, (width, width), 0)
        col_index = lax.broadcasted_iota(jnp.int32, (width, width), 1)
        below = jnp.where(row_index < col_index, 1.0, 0.0).astype(BF16)
        above = jnp.where(row_index < col_index, 0.0, 1.0).astype(BF16)
        start = pl.multiple_of(tm_pos * width, width)
        for mom in range(moms):
            for one in copies(mom):
                one.wait()
            for part in range(4):
                cols = pl.ds(part * width, width)
                block = out_ref[mom, pl.ds(start, width), cols]
                out_ref[mom, pl.ds(start, width), cols] = block * below
                out_ref[mom, pl.ds(rows, width), cols] = block * above

    vmem = pl.BlockSpec(memory_space=pltpu.VMEM)
    hbm = pl.BlockSpec(memory_space=pltpu.HBM)
    return pl.pallas_call(
        body,
        out_shape=(
            pltpu.VMEM((moms, rows + width, 4 * width), BF16),
            jax.ShapeDtypeStruct((2 * sites, 6 * count), BF16),
            jax.ShapeDtypeStruct((2 * moms, 6 * sites), BF16),
            jax.ShapeDtypeStruct((moms, width), F32),
        ),
        in_specs=[hbm, hbm, vmem],
        out_specs=(vmem, vmem, vmem, vmem),
        scratch_shapes=[pltpu.VMEM((2 * sites, 2 * count), F32), pltpu.SemaphoreType.DMA((moms, 4))],
        compiler_params=pltpu.CompilerParams(vmem_limit_bytes=4 * MIB),
        name="prepare",
    )(
        pltpu.with_memory_space_constraint(hist_less, pltpu.HBM),
        pltpu.with_memory_space_constraint(hist_great, pltpu.HBM),
        mom_table.reshape(1, count),
    )


def self_energy(pieces, forward, backward, count, slots):
    _, moms, width = pieces[0].shape
    sites = forward.shape[0] // 2
    rows_out = 4 * moms

    def body(*refs):
        piece_refs = refs[: len(pieces)]
        forward_ref, backward_ref, out_ref, rows_ref = refs[len(pieces) :]
        mom_pos = lax.axis_index("mom")
        for step, ref in enumerate(piece_refs):
            place = jnp.bitwise_xor(mom_pos, step) * moms
            for comp in range(4):
                start = pl.multiple_of(place + (comp % 2) * count, moms)
                rows_ref[pl.ds(start, moms), pl.ds((comp // 2) * width, width)] = ref[comp]
        rows = rows_ref[...]
        grid = three_products(forward_ref[...], rows) * (1.0 / count)
        less_real, less_imag = grid[:sites, :width], grid[sites:, :width]
        great_real, great_imag = grid[:sites, width:], grid[sites:, width:]
        scale = -coupling * coupling
        less_sq_real = less_real * less_real - less_imag * less_imag
        less_sq_imag = 2.0 * less_real * less_imag
        great_sq_real = great_real * great_real - great_imag * great_imag
        great_sq_imag = 2.0 * great_real * great_imag
        sig_less_real = scale * (less_sq_real * great_real + less_sq_imag * great_imag)
        sig_less_imag = scale * (less_sq_imag * great_real - less_sq_real * great_imag)
        sig_great_real = scale * (great_sq_real * less_real + great_sq_imag * less_imag)
        sig_great_imag = scale * (great_sq_imag * less_real - great_sq_real * less_imag)
        site = jnp.concatenate(
            [
                jnp.concatenate([sig_less_real, sig_great_real], axis=1),
                jnp.concatenate([sig_less_imag, sig_great_imag], axis=1),
            ],
            axis=0,
        )
        sig = three_products(backward_ref[...], site)
        packed = jnp.concatenate([sig[:, :width], sig[:, width:]], axis=0).astype(BF16)
        squares = rows[:, :width] * rows[:, :width]
        last = lax.broadcasted_iota(jnp.int32, squares.shape, 1) == width - 1
        density = jnp.sum(jnp.where(last, squares, 0.0), keepdims=True) / count
        high = density.astype(BF16).astype(F32)
        middle = (density - high).astype(BF16).astype(F32)
        low = density - high - middle
        row_index = lax.broadcasted_iota(jnp.int32, (EXTRA, width), 0)
        tail = jnp.where(row_index == 0, high, jnp.where(row_index == 1, middle, low)).astype(BF16)
        for slot in range(slots):
            out_ref[slot, :rows_out, :] = packed
            out_ref[slot, rows_out:, :] = tail

    vmem = pl.BlockSpec(memory_space=pltpu.VMEM)
    return pl.pallas_call(
        body,
        out_shape=jax.ShapeDtypeStruct((slots, rows_out + EXTRA, width), BF16),
        in_specs=[vmem] * (len(pieces) + 2),
        out_specs=vmem,
        scratch_shapes=[pltpu.VMEM((2 * count, 2 * width), F32)],
        compiler_params=pltpu.CompilerParams(vmem_limit_bytes=8 * MIB),
        name="self_energy",
    )(*pieces, forward, backward)


def turn(values):
    return [values[1], -values[0], values[3], -values[2]]


def rotate(values, phases):
    cos_part = jnp.cos(phases)
    sin_part = jnp.sin(phases)
    return [
        cos_part * values[0] + sin_part * values[1],
        cos_part * values[1] - sin_part * values[0],
        cos_part * values[2] + sin_part * values[3],
        cos_part * values[3] - sin_part * values[2],
    ]


def advance(received, history, energy, current, kept, last=False):
    slots, _, width = received.shape
    moms = history.shape[0]
    rows = slots * width
    first = kept is None

    def body(*refs):
        recv_ref, hist_ref, energy_ref, cur_ref = refs[:4]
        if first:
            trial_ref, keep_ref, dens_ref, lhs_ref = refs[4:]
            trial_refs = (trial_ref,)
        else:
            keep_ref, dens_ref = refs[4:6]
            trial_refs, lhs_ref = refs[6:-1], refs[-1]
        tm_pos = lax.axis_index("tm")
        for slot in range(slots):
            block = recv_ref[slot, : 4 * moms, :]
            low = jnp.where(slot <= tm_pos, 1.0, 0.0).astype(BF16)
            upp = jnp.where(slot > tm_pos, 1.0, 0.0).astype(BF16)
            cols = pl.ds(slot * width, width)
            lhs_ref[: 4 * moms, cols] = block * low
            lhs_ref[4 * moms :, cols] = block * upp
        own = recv_ref[tm_pos, : 4 * moms, :]
        lhs_ref[: 4 * moms, rows:] = jnp.zeros_like(own)
        lhs_ref[4 * moms :, rows:] = own
        lhs = lhs_ref[...]
        row_mom = lax.broadcasted_iota(jnp.int32, (8 * moms, 1), 0) % moms
        total = None
        for mom in range(moms):
            mask = jnp.where(row_mom == mom, 1.0, 0.0).astype(BF16)
            prod = jnp.dot(lhs * mask, hist_ref[mom], preferred_element_type=F32)
            total = prod if total is None else total + prod

        def pick(half, comp, col):
            start = (4 * half + comp) * moms
            return total[start : start + moms, col * width : (col + 1) * width]

        def product(half, comp, col):
            real = pick(half, comp, col) - pick(half, comp + 1, col + 1)
            imag = pick(half, comp, col + 1) + pick(half, comp + 1, col)
            return real, imag

        low_gl = product(0, 2, 0)
        low_lg = product(0, 0, 2)
        upp_gl = product(1, 2, 0)
        upp_ll = product(1, 0, 0)
        upp_gg = product(1, 2, 2)
        upp_lg = product(1, 0, 2)
        memory = [low_gl[i] - low_lg[i] + upp_gl[i] - upp_ll[i] for i in range(2)]
        memory += [low_gl[i] - low_lg[i] + upp_gg[i] - upp_lg[i] for i in range(2)]
        tail = recv_ref[slots - 1, 4 * moms :, :].astype(F32)
        density = tail[0:1] + tail[1:2] + tail[2:3]
        current = [cur_ref[i] for i in range(4)]
        if first:
            phases = (energy_ref[...] + coupling * density) * time_step
            turned = turn(memory)
            trial = rotate([current[i] + time_step * turned[i] for i in range(4)], phases)
            for i in range(4):
                keep_ref[i] = memory[i]
            dens_ref[...] = jnp.broadcast_to(density, dens_ref.shape)
        else:
            phases = (energy_ref[...] + coupling * 0.5 * (dens_ref[0:1] + density)) * time_step
            kept_turn = turn([keep_ref[i] for i in range(4)])
            turned = turn(memory)
            half = 0.5 * time_step
            trial = rotate([current[i] + half * kept_turn[i] for i in range(4)], phases)
            trial = [trial[i] + half * turned[i] for i in range(4)]
        for i in range(4):
            if last:
                trial_refs[i // 2][i % 2] = trial[i]
            else:
                trial_refs[0][i] = trial[i]

    vmem = pl.BlockSpec(memory_space=pltpu.VMEM)
    row_shape = jax.ShapeDtypeStruct((4, moms, width), F32)
    history = pltpu.with_memory_space_constraint(history, pltpu.VMEM)
    operands = [received, history, energy, current]
    shapes = [jax.ShapeDtypeStruct((2, moms, width), F32)] * 2 if last else [row_shape]
    if first:
        shapes += [row_shape, jax.ShapeDtypeStruct((8, width), F32)]
    else:
        operands += list(kept)
    return pl.pallas_call(
        body,
        out_shape=tuple(shapes),
        in_specs=[vmem] * len(operands),
        out_specs=tuple([vmem] * len(shapes)),
        scratch_shapes=[pltpu.VMEM((8 * moms, rows + width), BF16)],
        compiler_params=pltpu.CompilerParams(vmem_limit_bytes=16 * MIB),
        name="advance",
    )(*operands)


def per_device(hist_less, hist_great, row_less, row_great, mom_table):
    moms, width = row_less.shape[1:]
    mom_count = lax.axis_size("mom")
    time_count = lax.axis_size("tm")
    count = moms * mom_count
    history, forward, backward, energy = prepare(hist_less, hist_great, mom_table, mom_count)

    def evaluate(trial):
        pieces = [trial]
        for step in range(1, mom_count):
            pairs = [(i, i ^ step) for i in range(mom_count)]
            pieces.append(lax.ppermute(trial, "mom", pairs))
        sent = self_energy(pieces, forward, backward, count, time_count)
        return lax.all_to_all(sent, "tm", 0, 0)

    current = jnp.concatenate([row_less, row_great], axis=0)
    for index_new in range(NEW):
        trial, memory, density = advance(evaluate(current), history, energy, current, None)
        for index_pass in range(PASS):
            last = (index_new, index_pass) == (NEW - 1, PASS - 1)
            made = advance(evaluate(trial), history, energy, current, (memory, density), last)
            trial = made[0]
        current = trial
    return made


def solution(mesh):
    return jax.shard_map(
        per_device,
        mesh=mesh,
        in_specs=(
            P(None, "mom", None, "tm"),
            P(None, "mom", None, "tm"),
            P(None, "mom", "tm"),
            P(None, "mom", "tm"),
            P(),
        ),
        out_specs=(P(None, "mom", "tm"), P(None, "mom", "tm")),
        check_vma=False,
    )
```

```python
import math

import jax
import jax.numpy as jnp
from jax import lax
from jax.experimental import pallas as pl
from jax.experimental.pallas import tpu as pltpu
from jax.sharding import PartitionSpec as P

LSIDE = 8
NEW = 2
PASS = 2

coupling = 1.0
time_step = 0.08

F32 = jnp.float32
BF16 = jnp.bfloat16
LANES = 128
EXTRA = 16
MIB = 1 << 20


def split_two(values):
    high = values.astype(BF16)
    return high, (values - high.astype(F32)).astype(BF16)


def three_products(table, block):
    high, low = split_two(block)
    return jnp.dot(table, jnp.concatenate([high, low, high], axis=0), preferred_element_type=F32)


def prepare(hist_less, hist_great, mom_table, mom_count):
    _, moms, _, width = hist_less.shape
    count = moms * mom_count
    sites = LSIDE * LSIDE
    factor = 2.0 * math.pi / LSIDE

    def body(less_ref, great_ref, list_ref, out_ref, forward_ref, backward_ref, energy_ref, *scratch):
        block_ref, table_ref, mom_ref, sems = scratch
        tm_pos = lax.axis_index("tm")
        mom_pos = lax.axis_index("mom")

        start = pl.multiple_of(tm_pos * width, width)
        copies = []
        for which, ref in enumerate((less_ref, great_ref)):
            for part in range(2):
                copies.append(
                    pltpu.make_async_copy(
                        ref.at[part, :, pl.ds(start, width), :],
                        block_ref.at[2 * which + part],
                        sems.at[2 * which + part],
                    )
                )
        listed = pltpu.make_async_copy(list_ref, mom_ref, sems.at[4])
        for one in [listed, *copies]:
            one.start()
        listed.wait()

        moms_row = mom_ref[...]
        own_index = lax.broadcasted_iota(jnp.int32, (moms, count), 0) + mom_pos * moms
        own_lane = lax.broadcasted_iota(jnp.int32, (moms, count), 1)
        moms_own = jnp.sum(jnp.where(own_index == own_lane, moms_row.astype(F32), 0.0), axis=1, keepdims=True)
        moms_own = moms_own.astype(jnp.int32)

        def split_index(index):
            return lax.div(index, LSIDE).astype(F32), lax.rem(index, LSIDE).astype(F32)

        def store_split(out, table):
            high = table.astype(BF16)
            low = (table - high.astype(F32)).astype(BF16)
            depth = table.shape[1]
            out[:, :depth] = high
            out[:, depth : 2 * depth] = high
            out[:, 2 * depth :] = low

        site_x, site_y = split_index(lax.broadcasted_iota(jnp.int32, (sites, count), 0))
        mom_x, mom_y = split_index(jnp.broadcast_to(moms_row, (sites, count)))
        phase = factor * (site_x * mom_x + site_y * mom_y)
        cos_tab, sin_tab = jnp.cos(phase), jnp.sin(phase)
        table_ref[:sites, :count] = cos_tab
        table_ref[:sites, count:] = -sin_tab
        table_ref[sites:, :count] = sin_tab
        table_ref[sites:, count:] = cos_tab
        store_split(forward_ref, table_ref[...])
        site_x, site_y = split_index(lax.broadcasted_iota(jnp.int32, (moms, sites), 1))
        mom_x, mom_y = split_index(jnp.broadcast_to(moms_own, (moms, sites)))
        phase = factor * (site_x * mom_x + site_y * mom_y)
        cos_tab, sin_tab = jnp.cos(phase), jnp.sin(phase)
        table_ref[:moms, :sites] = cos_tab
        table_ref[:moms, sites:] = sin_tab
        table_ref[moms : 2 * moms, :sites] = -sin_tab
        table_ref[moms : 2 * moms, sites:] = cos_tab
        store_split(backward_ref, table_ref[: 2 * moms, :])
        mom_x, mom_y = split_index(jnp.broadcast_to(moms_own, (moms, width)))
        energy_ref[...] = -2.0 * (jnp.cos(factor * mom_x) + jnp.cos(factor * mom_y))

        row_index = lax.broadcasted_iota(jnp.int32, (width, width), 0)
        col_index = lax.broadcasted_iota(jnp.int32, (width, width), 1)
        for one in copies:
            one.wait()
        for mom in range(moms):
            for part in range(2):
                change = block_ref[part, mom].astype(F32) - block_ref[2 + part, mom].astype(F32)
                change = jnp.where(row_index < col_index, 0.0, change).astype(BF16)
                out_ref[pl.ds(mom * width, width), pl.ds(part * width, width)] = change

    vmem = pl.BlockSpec(memory_space=pltpu.VMEM)
    hbm = pl.BlockSpec(memory_space=pltpu.HBM)
    return pl.pallas_call(
        body,
        out_shape=(
            pltpu.VMEM((moms * width, 2 * width), BF16),
            jax.ShapeDtypeStruct((2 * sites, 6 * count), BF16),
            jax.ShapeDtypeStruct((2 * moms, 6 * sites), BF16),
            jax.ShapeDtypeStruct((moms, width), F32),
        ),
        in_specs=[hbm, hbm, hbm],
        out_specs=(vmem, vmem, vmem, vmem),
        scratch_shapes=[
            pltpu.VMEM((4, moms, width, width), BF16),
            pltpu.VMEM((2 * sites, 2 * count), F32),
            pltpu.VMEM((1, count), jnp.int32),
            pltpu.SemaphoreType.DMA((5,)),
        ],
        compiler_params=pltpu.CompilerParams(vmem_limit_bytes=8 * MIB),
        name="prepare",
    )(
        pltpu.with_memory_space_constraint(hist_less, pltpu.HBM),
        pltpu.with_memory_space_constraint(hist_great, pltpu.HBM),
        pltpu.with_memory_space_constraint(mom_table.reshape(1, count), pltpu.HBM),
    )


def self_energy(pieces, forward, backward, count, slots):
    _, moms, width = pieces[0].shape
    sites = forward.shape[0] // 2
    rows_out = 4 * moms

    def body(*refs):
        piece_refs = refs[: len(pieces)]
        forward_ref, backward_ref, out_ref, rows_ref = refs[len(pieces) :]
        mom_pos = lax.axis_index("mom")
        for step, ref in enumerate(piece_refs):
            place = jnp.bitwise_xor(mom_pos, step) * moms
            for comp in range(4):
                start = pl.multiple_of(place + (comp % 2) * count, moms)
                rows_ref[pl.ds(start, moms), pl.ds((comp // 2) * width, width)] = ref[comp]
        rows = rows_ref[...]
        grid = three_products(forward_ref[...], rows) * (1.0 / count)
        less_real, less_imag = grid[:sites, :width], grid[sites:, :width]
        great_real, great_imag = grid[:sites, width:], grid[sites:, width:]
        scale = -coupling * coupling
        less_sq_real = less_real * less_real - less_imag * less_imag
        less_sq_imag = 2.0 * less_real * less_imag
        great_sq_real = great_real * great_real - great_imag * great_imag
        great_sq_imag = 2.0 * great_real * great_imag
        sig_less_real = scale * (less_sq_real * great_real + less_sq_imag * great_imag)
        sig_less_imag = scale * (less_sq_imag * great_real - less_sq_real * great_imag)
        sig_great_real = scale * (great_sq_real * less_real + great_sq_imag * less_imag)
        sig_great_imag = scale * (great_sq_imag * less_real - great_sq_real * less_imag)
        site = jnp.concatenate(
            [
                jnp.concatenate([sig_less_real, sig_great_real], axis=1),
                jnp.concatenate([sig_less_imag, sig_great_imag], axis=1),
            ],
            axis=0,
        )
        sig = three_products(backward_ref[...], site)
        packed = jnp.concatenate([sig[:, :width], sig[:, width:]], axis=0).astype(BF16)
        squares = rows[:, :width] * rows[:, :width]
        last = lax.broadcasted_iota(jnp.int32, squares.shape, 1) == width - 1
        density = jnp.sum(jnp.where(last, squares, 0.0), keepdims=True) / count
        high = density.astype(BF16).astype(F32)
        middle = (density - high).astype(BF16).astype(F32)
        low = density - high - middle
        row_index = lax.broadcasted_iota(jnp.int32, (EXTRA, width), 0)
        tail = jnp.where(row_index == 0, high, jnp.where(row_index == 1, middle, low)).astype(BF16)
        for slot in range(slots):
            out_ref[slot, :rows_out, :] = packed
            out_ref[slot, rows_out:, :] = tail

    vmem = pl.BlockSpec(memory_space=pltpu.VMEM)
    return pl.pallas_call(
        body,
        out_shape=jax.ShapeDtypeStruct((slots, rows_out + EXTRA, width), BF16),
        in_specs=[vmem] * (len(pieces) + 2),
        out_specs=vmem,
        scratch_shapes=[pltpu.VMEM((2 * count, 2 * width), F32)],
        compiler_params=pltpu.CompilerParams(vmem_limit_bytes=8 * MIB),
        name="self_energy",
    )(*pieces, forward, backward)


def turn(values):
    return [values[1], -values[0], values[3], -values[2]]


def rotate(values, phases):
    cos_part = jnp.cos(phases)
    sin_part = jnp.sin(phases)
    return [
        cos_part * values[0] + sin_part * values[1],
        cos_part * values[1] - sin_part * values[0],
        cos_part * values[2] + sin_part * values[3],
        cos_part * values[3] - sin_part * values[2],
    ]


def advance(received, history, energy, current, kept, last=False):
    slots, _, width = received.shape
    moms = energy.shape[0]
    rows = slots * width
    first = kept is None
    span = 4 * moms

    def body(*refs):
        recv_ref, less_ref, great_ref, diag_ref, energy_ref, cur_ref = refs[:6]
        if first:
            trial_ref, keep_ref, dens_ref, lhs_ref = refs[6:]
            trial_refs = (trial_ref,)
        else:
            keep_ref, dens_ref = refs[6:8]
            trial_refs, lhs_ref = refs[8:-1], refs[-1]
        tm_pos = lax.axis_index("tm")
        for slot in range(slots):
            block = recv_ref[slot, :span, :]
            low = jnp.where(slot <= tm_pos, 1.0, 0.0).astype(BF16)
            upp = jnp.where(slot > tm_pos, 1.0, 0.0).astype(BF16)
            cols = pl.ds(slot * width, width)
            lhs_ref[:span, cols] = block * low
            lhs_ref[span:, cols] = block * upp
        own = recv_ref[tm_pos, :span, :]
        lhs = lhs_ref[...]
        row_mom = lax.broadcasted_iota(jnp.int32, (2 * span, 1), 0) % moms
        masks = [jnp.where(row_mom == mom, 1.0, 0.0).astype(BF16) for mom in range(moms)]
        spread = jnp.concatenate([own * mask[:span] for mask in masks], axis=1)
        change = jnp.dot(spread, diag_ref[...], preferred_element_type=F32)
        total = None
        for mom in range(moms):
            main = [less_ref[0, mom], less_ref[1, mom], great_ref[0, mom], great_ref[1, mom]]
            prod = jnp.dot(lhs * masks[mom], jnp.concatenate(main, axis=1), preferred_element_type=F32)
            total = prod if total is None else total + prod

        def product(table, row, col):
            def pick(i, j):
                return table[(row + i) * moms : (row + i + 1) * moms, (col + j) * width : (col + j + 1) * width]

            return pick(0, 0) - pick(1, 1), pick(0, 1) + pick(1, 0)

        low_gl = product(total, 2, 0)
        low_lg = product(total, 0, 2)
        upp_gl = product(total, 6, 0)
        upp_ll = product(total, 4, 0)
        upp_gg = product(total, 6, 2)
        upp_lg = product(total, 4, 2)
        own_less = product(change, 0, 0)
        own_great = product(change, 2, 0)
        memory = [low_gl[i] - low_lg[i] + upp_gl[i] - upp_ll[i] - own_less[i] for i in range(2)]
        memory += [low_gl[i] - low_lg[i] + upp_gg[i] - upp_lg[i] - own_great[i] for i in range(2)]
        tail = recv_ref[slots - 1, 4 * moms :, :].astype(F32)
        density = tail[0:1] + tail[1:2] + tail[2:3]
        current = [cur_ref[i] for i in range(4)]
        if first:
            phases = (energy_ref[...] + coupling * density) * time_step
            turned = turn(memory)
            trial = rotate([current[i] + time_step * turned[i] for i in range(4)], phases)
            for i in range(4):
                keep_ref[i] = memory[i]
            dens_ref[...] = jnp.broadcast_to(density, dens_ref.shape)
        else:
            phases = (energy_ref[...] + coupling * 0.5 * (dens_ref[0:1] + density)) * time_step
            kept_turn = turn([keep_ref[i] for i in range(4)])
            turned = turn(memory)
            half = 0.5 * time_step
            trial = rotate([current[i] + half * kept_turn[i] for i in range(4)], phases)
            trial = [trial[i] + half * turned[i] for i in range(4)]
        for i in range(4):
            if last:
                trial_refs[i // 2][i % 2] = trial[i]
            else:
                trial_refs[0][i] = trial[i]

    vmem = pl.BlockSpec(memory_space=pltpu.VMEM)
    row_shape = jax.ShapeDtypeStruct((4, moms, width), F32)
    operands = [received, *history, energy, current]
    shapes = [jax.ShapeDtypeStruct((2, moms, width), F32)] * 2 if last else [row_shape]
    if first:
        shapes += [row_shape, jax.ShapeDtypeStruct((8, width), F32)]
    else:
        operands += list(kept)
    return pl.pallas_call(
        body,
        out_shape=tuple(shapes),
        in_specs=[vmem] * len(operands),
        out_specs=tuple([vmem] * len(shapes)),
        scratch_shapes=[pltpu.VMEM((2 * span, rows), BF16)],
        compiler_params=pltpu.CompilerParams(vmem_limit_bytes=16 * MIB),
        name="advance",
    )(*operands)


def per_device(hist_less, hist_great, row_less, row_great, mom_table):
    moms, width = row_less.shape[1:]
    mom_count = lax.axis_size("mom")
    time_count = lax.axis_size("tm")
    count = moms * mom_count
    diagonal, forward, backward, energy = prepare(hist_less, hist_great, mom_table, mom_count)
    history = [
        pltpu.with_memory_space_constraint(hist_less, pltpu.VMEM),
        pltpu.with_memory_space_constraint(hist_great, pltpu.VMEM),
        diagonal,
    ]

    def evaluate(trial):
        pieces = [trial]
        for step in range(1, mom_count):
            pairs = [(i, i ^ step) for i in range(mom_count)]
            pieces.append(lax.ppermute(trial, "mom", pairs))
        sent = self_energy(pieces, forward, backward, count, time_count)
        return lax.all_to_all(sent, "tm", 0, 0)

    current = jnp.pad(row_less, ((0, 2), (0, 0), (0, 0))) + jnp.pad(row_great, ((2, 0), (0, 0), (0, 0)))
    for index_new in range(NEW):
        trial, memory, density = advance(evaluate(current), history, energy, current, None)
        for index_pass in range(PASS):
            last = (index_new, index_pass) == (NEW - 1, PASS - 1)
            made = advance(evaluate(trial), history, energy, current, (memory, density), last)
            trial = made[0]
        current = trial
    return made


def solution(mesh):
    return jax.shard_map(
        per_device,
        mesh=mesh,
        in_specs=(
            P(None, "mom", None, "tm"),
            P(None, "mom", None, "tm"),
            P(None, "mom", "tm"),
            P(None, "mom", "tm"),
            P(),
        ),
        out_specs=(P(None, "mom", "tm"), P(None, "mom", "tm")),
        check_vma=False,
    )
```

```python
import math

import jax
import jax.numpy as jnp
from jax import lax
from jax.experimental import pallas as pl
from jax.experimental.pallas import tpu as pltpu
from jax.sharding import PartitionSpec as P

LSIDE = 8
NEW = 2
PASS = 2

coupling = 1.0
time_step = 0.08

F32 = jnp.float32
BF16 = jnp.bfloat16
LANES = 128
EXTRA = 16
MIB = 1 << 20


def split_two(values):
    high = values.astype(BF16)
    return high, (values - high.astype(F32)).astype(BF16)


def three_products(table, block):
    high, low = split_two(block)
    return jnp.dot(table, jnp.concatenate([high, low, high], axis=0), preferred_element_type=F32)


def prepare(hist_less, hist_great, mom_table, mom_count):
    _, moms, _, width = hist_less.shape
    count = moms * mom_count
    sites = LSIDE * LSIDE
    factor = 2.0 * math.pi / LSIDE

    def body(less_ref, great_ref, list_ref, out_ref, forward_ref, backward_ref, energy_ref, turn_ref, *scratch):
        block_ref, table_ref, mom_ref, sems = scratch
        tm_pos = lax.axis_index("tm")
        mom_pos = lax.axis_index("mom")

        start = pl.multiple_of(tm_pos * width, width)
        copies = []
        for which, ref in enumerate((less_ref, great_ref)):
            for part in range(2):
                copies.append(
                    pltpu.make_async_copy(
                        ref.at[part, :, pl.ds(start, width), :],
                        block_ref.at[2 * which + part],
                        sems.at[2 * which + part],
                    )
                )
        listed = pltpu.make_async_copy(list_ref, mom_ref, sems.at[4])
        for one in [listed, *copies]:
            one.start()
        listed.wait()

        moms_row = mom_ref[...]
        own_index = lax.broadcasted_iota(jnp.int32, (moms, count), 0) + mom_pos * moms
        own_lane = lax.broadcasted_iota(jnp.int32, (moms, count), 1)
        moms_own = jnp.sum(jnp.where(own_index == own_lane, moms_row.astype(F32), 0.0), axis=1, keepdims=True)
        moms_own = moms_own.astype(jnp.int32)

        def split_index(index):
            return lax.div(index, LSIDE).astype(F32), lax.rem(index, LSIDE).astype(F32)

        def store_split(out, table):
            high = table.astype(BF16)
            low = (table - high.astype(F32)).astype(BF16)
            depth = table.shape[1]
            out[:, :depth] = high
            out[:, depth : 2 * depth] = high
            out[:, 2 * depth :] = low

        site_x, site_y = split_index(lax.broadcasted_iota(jnp.int32, (sites, count), 0))
        mom_x, mom_y = split_index(jnp.broadcast_to(moms_row, (sites, count)))
        phase = factor * (site_x * mom_x + site_y * mom_y)
        cos_tab, sin_tab = jnp.cos(phase), jnp.sin(phase)
        table_ref[:sites, :count] = cos_tab
        table_ref[:sites, count:] = -sin_tab
        table_ref[sites:, :count] = sin_tab
        table_ref[sites:, count:] = cos_tab
        store_split(forward_ref, table_ref[...])
        site_x, site_y = split_index(lax.broadcasted_iota(jnp.int32, (moms, sites), 1))
        mom_x, mom_y = split_index(jnp.broadcast_to(moms_own, (moms, sites)))
        phase = factor * (site_x * mom_x + site_y * mom_y)
        cos_tab, sin_tab = jnp.cos(phase), jnp.sin(phase)
        table_ref[:moms, :sites] = cos_tab
        table_ref[:moms, sites:] = sin_tab
        table_ref[moms : 2 * moms, :sites] = -sin_tab
        table_ref[moms : 2 * moms, sites:] = cos_tab
        store_split(backward_ref, table_ref[: 2 * moms, :])
        mom_x, mom_y = split_index(jnp.broadcast_to(moms_own, (moms, width)))
        energy_ref[...] = -2.0 * (jnp.cos(factor * mom_x) + jnp.cos(factor * mom_y))
        row_index = lax.broadcasted_iota(jnp.int32, (count, count), 0)
        col_index = lax.broadcasted_iota(jnp.int32, (count, count), 1)
        moms_col = jnp.sum(jnp.where(row_index == col_index, moms_row.astype(F32), 0.0), axis=1, keepdims=True)
        mom_x, mom_y = split_index(jnp.broadcast_to(moms_col.astype(jnp.int32), (count, width)))
        angle = -2.0 * time_step * (jnp.cos(factor * mom_x) + jnp.cos(factor * mom_y))
        turn_ref[0] = jnp.cos(angle)
        turn_ref[1] = jnp.sin(angle)

        row_index = lax.broadcasted_iota(jnp.int32, (width, width), 0)
        col_index = lax.broadcasted_iota(jnp.int32, (width, width), 1)
        for one in copies:
            one.wait()
        for mom in range(moms):
            for part in range(2):
                change = block_ref[part, mom].astype(F32) - block_ref[2 + part, mom].astype(F32)
                change = jnp.where(row_index < col_index, 0.0, change).astype(BF16)
                out_ref[pl.ds(mom * width, width), pl.ds(part * width, width)] = change

    vmem = pl.BlockSpec(memory_space=pltpu.VMEM)
    hbm = pl.BlockSpec(memory_space=pltpu.HBM)
    return pl.pallas_call(
        body,
        out_shape=(
            pltpu.VMEM((moms * width, 2 * width), BF16),
            jax.ShapeDtypeStruct((2 * sites, 6 * count), BF16),
            jax.ShapeDtypeStruct((2 * moms, 6 * sites), BF16),
            jax.ShapeDtypeStruct((moms, width), F32),
            jax.ShapeDtypeStruct((2, count, width), F32),
        ),
        in_specs=[hbm, hbm, hbm],
        out_specs=(vmem, vmem, vmem, vmem, vmem),
        scratch_shapes=[
            pltpu.VMEM((4, moms, width, width), BF16),
            pltpu.VMEM((2 * sites, 2 * count), F32),
            pltpu.VMEM((1, count), jnp.int32),
            pltpu.SemaphoreType.DMA((5,)),
        ],
        compiler_params=pltpu.CompilerParams(vmem_limit_bytes=8 * MIB),
        name="prepare",
    )(
        pltpu.with_memory_space_constraint(hist_less, pltpu.HBM),
        pltpu.with_memory_space_constraint(hist_great, pltpu.HBM),
        pltpu.with_memory_space_constraint(mom_table.reshape(1, count), pltpu.HBM),
    )


def self_energy(kind, pieces, tables, state, slots):
    forward, backward, waves = tables
    _, moms, width = pieces[0].shape
    sites = forward.shape[0] // 2
    count = waves.shape[1]
    rows_out = 4 * moms
    keeps = kind != "correct"

    def body(*refs):
        piece_refs = refs[: len(pieces)]
        forward_ref, backward_ref, waves_ref, *refs = refs[len(pieces) :]
        state_refs, refs = refs[: len(state)], refs[len(state) :]
        out_ref, rows_ref = refs[0], refs[-1]
        mom_pos = lax.axis_index("mom")
        for step, ref in enumerate(piece_refs):
            place = jnp.bitwise_xor(mom_pos, step) * moms
            for comp in range(4):
                start = pl.multiple_of(place + (comp % 2) * count, moms)
                rows_ref[pl.ds(start, moms), pl.ds((comp // 2) * width, width)] = ref[comp].astype(F32)
        rows = rows_ref[...]
        if kind == "start":
            refs[1][...] = rows
        else:
            wave_ref = state_refs[-1]
            cos_one, sin_one = wave_ref[0:1], wave_ref[1:2]
            cos_part = waves_ref[0] * cos_one - waves_ref[1] * sin_one
            sin_part = waves_ref[1] * cos_one + waves_ref[0] * sin_one
            cos_part = jnp.concatenate([cos_part, cos_part], axis=1)
            sin_part = jnp.concatenate([sin_part, sin_part], axis=1)
            base_real, base_imag = state_refs[0][:count], state_refs[0][count:]
            new_real, new_imag = rows[:count], rows[count:]
            if kind == "predict":
                refs[1][...] = rows
                base_real, base_imag = base_real + time_step * new_imag, base_imag - time_step * new_real
            else:
                half = 0.5 * time_step
                kept_ref = state_refs[1]
                base_real, base_imag = base_real + half * kept_ref[count:], base_imag - half * kept_ref[:count]
            real = cos_part * base_real + sin_part * base_imag
            imag = cos_part * base_imag - sin_part * base_real
            if kind != "predict":
                real, imag = real + half * new_imag, imag - half * new_real
            rows = jnp.concatenate([real, imag], axis=0)
            if kind == "finish":
                refs[1][...] = rows
        grid = three_products(forward_ref[...], rows) * (1.0 / count)
        less_real, less_imag = grid[:sites, :width], grid[sites:, :width]
        great_real, great_imag = grid[:sites, width:], grid[sites:, width:]
        scale = -coupling * coupling
        less_sq_real = less_real * less_real - less_imag * less_imag
        less_sq_imag = 2.0 * less_real * less_imag
        great_sq_real = great_real * great_real - great_imag * great_imag
        great_sq_imag = 2.0 * great_real * great_imag
        sig_less_real = scale * (less_sq_real * great_real + less_sq_imag * great_imag)
        sig_less_imag = scale * (less_sq_imag * great_real - less_sq_real * great_imag)
        sig_great_real = scale * (great_sq_real * less_real + great_sq_imag * less_imag)
        sig_great_imag = scale * (great_sq_imag * less_real - great_sq_real * less_imag)
        site = jnp.concatenate(
            [
                jnp.concatenate([sig_less_real, sig_great_real], axis=1),
                jnp.concatenate([sig_less_imag, sig_great_imag], axis=1),
            ],
            axis=0,
        )
        sig = three_products(backward_ref[...], site)
        packed = jnp.concatenate([sig[:, :width], sig[:, width:]], axis=0).astype(BF16)
        squares = rows[:, :width] * rows[:, :width]
        last = lax.broadcasted_iota(jnp.int32, squares.shape, 1) == width - 1
        density = jnp.sum(jnp.where(last, squares, 0.0), keepdims=True) / count
        high = density.astype(BF16).astype(F32)
        middle = (density - high).astype(BF16).astype(F32)
        low = density - high - middle
        row_index = lax.broadcasted_iota(jnp.int32, (EXTRA, width), 0)
        tail = jnp.where(row_index == 0, high, jnp.where(row_index == 1, middle, low)).astype(BF16)
        for slot in range(slots):
            out_ref[slot, :rows_out, :] = packed
            out_ref[slot, rows_out:, :] = tail

    vmem = pl.BlockSpec(memory_space=pltpu.VMEM)
    operands = [*pieces, *tables, *state]
    shapes = [jax.ShapeDtypeStruct((slots, rows_out + EXTRA, width), BF16)]
    if keeps:
        shapes.append(jax.ShapeDtypeStruct((2 * count, 2 * width), F32))
    return pl.pallas_call(
        body,
        out_shape=tuple(shapes),
        in_specs=[vmem] * len(operands),
        out_specs=tuple([vmem] * len(shapes)),
        scratch_shapes=[pltpu.VMEM((2 * count, 2 * width), F32)],
        compiler_params=pltpu.CompilerParams(vmem_limit_bytes=8 * MIB),
        name="self_energy",
    )(*operands)


def turn(values):
    return [values[1], -values[0], values[3], -values[2]]


def rotate(values, phases):
    cos_part = jnp.cos(phases)
    sin_part = jnp.sin(phases)
    return [
        cos_part * values[0] + sin_part * values[1],
        cos_part * values[1] - sin_part * values[0],
        cos_part * values[2] + sin_part * values[3],
        cos_part * values[3] - sin_part * values[2],
    ]


def advance(received, history, moms, wave, final=None):
    slots, _, width = received.shape
    rows = slots * width
    span = 4 * moms

    def body(*refs):
        recv_ref, less_ref, great_ref, diag_ref, *refs, lhs_ref = refs
        tm_pos = lax.axis_index("tm")
        for slot in range(slots):
            block = recv_ref[slot, :span, :]
            low = jnp.where(slot <= tm_pos, 1.0, 0.0).astype(BF16)
            upp = jnp.where(slot > tm_pos, 1.0, 0.0).astype(BF16)
            cols = pl.ds(slot * width, width)
            lhs_ref[:span, cols] = block * low
            lhs_ref[span:, cols] = block * upp
        own = recv_ref[tm_pos, :span, :]
        lhs = lhs_ref[...]
        row_mom = lax.broadcasted_iota(jnp.int32, (2 * span, 1), 0) % moms
        masks = [jnp.where(row_mom == mom, 1.0, 0.0).astype(BF16) for mom in range(moms)]
        spread = jnp.concatenate([own * mask[:span] for mask in masks], axis=1)
        change = jnp.dot(spread, diag_ref[...], preferred_element_type=F32)
        total = None
        for mom in range(moms):
            main = [less_ref[0, mom], less_ref[1, mom], great_ref[0, mom], great_ref[1, mom]]
            prod = jnp.dot(lhs * masks[mom], jnp.concatenate(main, axis=1), preferred_element_type=F32)
            total = prod if total is None else total + prod

        def product(table, row, col):
            def pick(i, j):
                return table[(row + i) * moms : (row + i + 1) * moms, (col + j) * width : (col + j + 1) * width]

            return pick(0, 0) - pick(1, 1), pick(0, 1) + pick(1, 0)

        low_gl = product(total, 2, 0)
        low_lg = product(total, 0, 2)
        upp_gl = product(total, 6, 0)
        upp_ll = product(total, 4, 0)
        upp_gg = product(total, 6, 2)
        upp_lg = product(total, 4, 2)
        own_less = product(change, 0, 0)
        own_great = product(change, 2, 0)
        memory = [low_gl[i] - low_lg[i] + upp_gl[i] - upp_ll[i] - own_less[i] for i in range(2)]
        memory += [low_gl[i] - low_lg[i] + upp_gg[i] - upp_lg[i] - own_great[i] for i in range(2)]
        tail = recv_ref[slots - 1, 4 * moms :, :].astype(F32)
        density = tail[0:1] + tail[1:2] + tail[2:3]
        mean = density if wave is None else 0.5 * (refs[0][2:3] + density)
        if final is None:
            full_ref, sent_ref, wave_ref = refs[-3:]
            for i in range(4):
                full_ref[i] = memory[i]
                sent_ref[i] = memory[i].astype(BF16)
            phase = (coupling * time_step) * mean
            wave_ref[0:1] = jnp.cos(phase)
            wave_ref[1:2] = jnp.sin(phase)
            wave_ref[2:] = jnp.broadcast_to(density, (6, width))
        else:
            energy_ref, row_ref, kept_ref = refs[1:4]
            mom_pos = lax.axis_index("mom")
            half = 0.5 * time_step
            kept_turn = turn([kept_ref[i] for i in range(4)])
            turned = turn(memory)
            current = []
            for i in range(4):
                start = pl.multiple_of(mom_pos * moms + (i % 2) * (row_ref.shape[0] // 2), moms)
                current.append(row_ref[pl.ds(start, moms), (i // 2) * width : (i // 2 + 1) * width])
            phases = (energy_ref[...] + coupling * mean) * time_step
            trial = rotate([current[i] + half * kept_turn[i] for i in range(4)], phases)
            for i in range(4):
                refs[4 + i // 2][i % 2] = trial[i] + half * turned[i]

    vmem = pl.BlockSpec(memory_space=pltpu.VMEM)
    operands = [received, *history]
    if wave is not None:
        operands.append(wave)
    if final is None:
        block = (4, moms, width)
        shapes = [jax.ShapeDtypeStruct(block, F32), jax.ShapeDtypeStruct(block, BF16)]
        shapes.append(jax.ShapeDtypeStruct((8, width), F32))
    else:
        operands += final
        shapes = [jax.ShapeDtypeStruct((2, moms, width), F32)] * 2
    return pl.pallas_call(
        body,
        out_shape=tuple(shapes),
        in_specs=[vmem] * len(operands),
        out_specs=tuple([vmem] * len(shapes)),
        scratch_shapes=[pltpu.VMEM((2 * span, rows), BF16)],
        compiler_params=pltpu.CompilerParams(vmem_limit_bytes=16 * MIB),
        name="advance",
    )(*operands)


def per_device(hist_less, hist_great, row_less, row_great, mom_table):
    moms, width = row_less.shape[1:]
    mom_count = lax.axis_size("mom")
    time_count = lax.axis_size("tm")
    diagonal, forward, backward, energy, waves = prepare(hist_less, hist_great, mom_table, mom_count)
    history = [
        pltpu.with_memory_space_constraint(hist_less, pltpu.VMEM),
        pltpu.with_memory_space_constraint(hist_great, pltpu.VMEM),
        diagonal,
    ]

    def evaluate(kind, own, sent, state, wave, final=None):
        pieces = [own]
        for step in range(1, mom_count):
            pairs = [(i, i ^ step) for i in range(mom_count)]
            pieces.append(lax.ppermute(sent, "mom", pairs))
        payload, *kept = self_energy(kind, pieces, (forward, backward, waves), state, time_count)
        return kept, advance(lax.all_to_all(payload, "tm", 0, 0), history, moms, wave, final)

    current = jnp.pad(row_less, ((0, 2), (0, 0), (0, 0))) + jnp.pad(row_great, ((2, 0), (0, 0), (0, 0)))
    (row,), (own, sent, wave) = evaluate("start", current, current, (), None)
    for index_new in range(NEW):
        start_own, start_wave = own, wave
        (kept,), (own, sent, wave) = evaluate("predict", own, sent, (row, wave), start_wave)
        for index_pass in range(1, PASS):
            final = (energy, row, start_own) if (index_new, index_pass) == (NEW - 1, PASS - 1) else None
            _, made = evaluate("correct", own, sent, (row, kept, wave), start_wave, final)
            if final is None:
                own, sent, wave = made
        if index_new + 1 < NEW:
            (row,), (own, sent, wave) = evaluate("finish", own, sent, (row, kept, wave), None)
    return made


def solution(mesh):
    return jax.shard_map(
        per_device,
        mesh=mesh,
        in_specs=(
            P(None, "mom", None, "tm"),
            P(None, "mom", None, "tm"),
            P(None, "mom", "tm"),
            P(None, "mom", "tm"),
            P(),
        ),
        out_specs=(P(None, "mom", "tm"), P(None, "mom", "tm")),
        check_vma=False,
    )
```

```python
import math

import jax
import jax.numpy as jnp
from jax import lax
from jax.experimental import pallas as pl
from jax.experimental.pallas import tpu as pltpu
from jax.sharding import PartitionSpec as P

LSIDE = 8
NEW = 2
PASS = 2

coupling = 1.0
time_step = 0.08

F32 = jnp.float32
BF16 = jnp.bfloat16
LANES = 128
EXTRA = 8
MIB = 1 << 20


def split_two(values):
    high = values.astype(BF16)
    return high, (values - high.astype(F32)).astype(BF16)


def three_products(table, block):
    high, low = split_two(block)
    return jnp.dot(table, jnp.concatenate([high, low, high], axis=0), preferred_element_type=F32)


def prepare(hist_less, hist_great, mom_table, mom_count):
    _, moms, _, width = hist_less.shape
    count = moms * mom_count
    sites = LSIDE * LSIDE
    factor = 2.0 * math.pi / LSIDE

    def body(less_ref, great_ref, list_ref, out_ref, forward_ref, backward_ref, energy_ref, turn_ref, *scratch):
        block_ref, table_ref, mom_ref, sems = scratch
        tm_pos = lax.axis_index("tm")
        mom_pos = lax.axis_index("mom")

        start = pl.multiple_of(tm_pos * width, width)
        copies = []
        for which, ref in enumerate((less_ref, great_ref)):
            for part in range(2):
                copies.append(
                    pltpu.make_async_copy(
                        ref.at[part, :, pl.ds(start, width), :],
                        block_ref.at[2 * which + part],
                        sems.at[2 * which + part],
                    )
                )
        listed = pltpu.make_async_copy(list_ref, mom_ref, sems.at[4])
        for one in [listed, *copies]:
            one.start()
        listed.wait()

        moms_row = mom_ref[...]
        own_index = lax.broadcasted_iota(jnp.int32, (moms, count), 0) + mom_pos * moms
        own_lane = lax.broadcasted_iota(jnp.int32, (moms, count), 1)
        moms_own = jnp.sum(jnp.where(own_index == own_lane, moms_row.astype(F32), 0.0), axis=1, keepdims=True)
        moms_own = moms_own.astype(jnp.int32)

        def split_index(index):
            return lax.div(index, LSIDE).astype(F32), lax.rem(index, LSIDE).astype(F32)

        def store_split(out, table):
            high = table.astype(BF16)
            low = (table - high.astype(F32)).astype(BF16)
            depth = table.shape[1]
            out[:, :depth] = high
            out[:, depth : 2 * depth] = high
            out[:, 2 * depth :] = low

        site_x, site_y = split_index(lax.broadcasted_iota(jnp.int32, (sites, count), 0))
        mom_x, mom_y = split_index(jnp.broadcast_to(moms_row, (sites, count)))
        phase = factor * (site_x * mom_x + site_y * mom_y)
        cos_tab, sin_tab = jnp.cos(phase), jnp.sin(phase)
        table_ref[:sites, :count] = cos_tab
        table_ref[:sites, count:] = -sin_tab
        table_ref[sites:, :count] = sin_tab
        table_ref[sites:, count:] = cos_tab
        store_split(forward_ref, table_ref[...])
        site_x, site_y = split_index(lax.broadcasted_iota(jnp.int32, (moms, sites), 1))
        mom_x, mom_y = split_index(jnp.broadcast_to(moms_own, (moms, sites)))
        phase = factor * (site_x * mom_x + site_y * mom_y)
        cos_tab, sin_tab = jnp.cos(phase), jnp.sin(phase)
        table_ref[:moms, :sites] = cos_tab
        table_ref[:moms, sites:] = sin_tab
        table_ref[moms : 2 * moms, :sites] = -sin_tab
        table_ref[moms : 2 * moms, sites:] = cos_tab
        store_split(backward_ref, table_ref[: 2 * moms, :])
        mom_x, mom_y = split_index(jnp.broadcast_to(moms_own, (moms, width)))
        energy_ref[...] = -2.0 * (jnp.cos(factor * mom_x) + jnp.cos(factor * mom_y))
        row_index = lax.broadcasted_iota(jnp.int32, (count, count), 0)
        col_index = lax.broadcasted_iota(jnp.int32, (count, count), 1)
        moms_col = jnp.sum(jnp.where(row_index == col_index, moms_row.astype(F32), 0.0), axis=1, keepdims=True)
        mom_x, mom_y = split_index(jnp.broadcast_to(moms_col.astype(jnp.int32), (count, width)))
        angle = -2.0 * time_step * (jnp.cos(factor * mom_x) + jnp.cos(factor * mom_y))
        turn_ref[0] = jnp.cos(angle)
        turn_ref[1] = jnp.sin(angle)

        row_index = lax.broadcasted_iota(jnp.int32, (width, width), 0)
        col_index = lax.broadcasted_iota(jnp.int32, (width, width), 1)
        for one in copies:
            one.wait()
        for mom in range(moms):
            for part in range(2):
                change = block_ref[part, mom].astype(F32) - block_ref[2 + part, mom].astype(F32)
                change = jnp.where(row_index < col_index, 0.0, change).astype(BF16)
                out_ref[pl.ds(mom * width, width), pl.ds(part * width, width)] = change

    vmem = pl.BlockSpec(memory_space=pltpu.VMEM)
    hbm = pl.BlockSpec(memory_space=pltpu.HBM)
    return pl.pallas_call(
        body,
        out_shape=(
            pltpu.VMEM((moms * width, 2 * width), BF16),
            jax.ShapeDtypeStruct((2 * sites, 6 * count), BF16),
            jax.ShapeDtypeStruct((2 * moms, 6 * sites), BF16),
            jax.ShapeDtypeStruct((moms, width), F32),
            jax.ShapeDtypeStruct((2, count, width), F32),
        ),
        in_specs=[hbm, hbm, hbm],
        out_specs=(vmem, vmem, vmem, vmem, vmem),
        scratch_shapes=[
            pltpu.VMEM((4, moms, width, width), BF16),
            pltpu.VMEM((2 * sites, 2 * count), F32),
            pltpu.VMEM((1, count), jnp.int32),
            pltpu.SemaphoreType.DMA((5,)),
        ],
        compiler_params=pltpu.CompilerParams(vmem_limit_bytes=8 * MIB),
        name="prepare",
    )(
        pltpu.with_memory_space_constraint(hist_less, pltpu.HBM),
        pltpu.with_memory_space_constraint(hist_great, pltpu.HBM),
        pltpu.with_memory_space_constraint(mom_table.reshape(1, count), pltpu.HBM),
    )


def self_energy(kind, pieces, tables, state, slots):
    forward, backward, waves = tables
    _, moms, width = pieces[0].shape
    sites = forward.shape[0] // 2
    count = waves.shape[1]
    rows_out = 4 * moms
    keeps = kind != "correct"

    def body(*refs):
        piece_refs = refs[: len(pieces)]
        forward_ref, backward_ref, waves_ref, *refs = refs[len(pieces) :]
        state_refs, refs = refs[: len(state)], refs[len(state) :]
        out_ref, rows_ref = refs[0], refs[-1]
        mom_pos = lax.axis_index("mom")
        for step, ref in enumerate(piece_refs):
            place = jnp.bitwise_xor(mom_pos, step) * moms
            for comp in range(4):
                start = pl.multiple_of(place + (comp % 2) * count, moms)
                rows_ref[pl.ds(start, moms), pl.ds((comp // 2) * width, width)] = ref[comp].astype(F32)
        rows = rows_ref[...]
        if kind == "start":
            refs[1][...] = rows
        else:
            wave_ref = state_refs[-1]
            cos_one, sin_one = wave_ref[0:1], wave_ref[1:2]
            cos_part = waves_ref[0] * cos_one - waves_ref[1] * sin_one
            sin_part = waves_ref[1] * cos_one + waves_ref[0] * sin_one
            cos_part = jnp.concatenate([cos_part, cos_part], axis=1)
            sin_part = jnp.concatenate([sin_part, sin_part], axis=1)
            base_real, base_imag = state_refs[0][:count], state_refs[0][count:]
            new_real, new_imag = rows[:count], rows[count:]
            if kind == "predict":
                refs[1][...] = rows
                base_real, base_imag = base_real + time_step * new_imag, base_imag - time_step * new_real
            else:
                half = 0.5 * time_step
                kept_ref = state_refs[1]
                base_real, base_imag = base_real + half * kept_ref[count:], base_imag - half * kept_ref[:count]
            real = cos_part * base_real + sin_part * base_imag
            imag = cos_part * base_imag - sin_part * base_real
            if kind != "predict":
                real, imag = real + half * new_imag, imag - half * new_real
            rows = jnp.concatenate([real, imag], axis=0)
            if kind == "finish":
                refs[1][...] = rows
        grid = three_products(forward_ref[...], rows) * (1.0 / count)
        less_real, less_imag = grid[:sites, :width], grid[sites:, :width]
        great_real, great_imag = grid[:sites, width:], grid[sites:, width:]
        scale = -coupling * coupling
        less_sq_real = less_real * less_real - less_imag * less_imag
        less_sq_imag = 2.0 * less_real * less_imag
        great_sq_real = great_real * great_real - great_imag * great_imag
        great_sq_imag = 2.0 * great_real * great_imag
        sig_less_real = scale * (less_sq_real * great_real + less_sq_imag * great_imag)
        sig_less_imag = scale * (less_sq_imag * great_real - less_sq_real * great_imag)
        sig_great_real = scale * (great_sq_real * less_real + great_sq_imag * less_imag)
        sig_great_imag = scale * (great_sq_imag * less_real - great_sq_real * less_imag)
        site = jnp.concatenate(
            [
                jnp.concatenate([sig_less_real, sig_great_real], axis=1),
                jnp.concatenate([sig_less_imag, sig_great_imag], axis=1),
            ],
            axis=0,
        )
        sig = three_products(backward_ref[...], site)
        packed = jnp.concatenate([sig[:, :width], sig[:, width:]], axis=0).astype(BF16)
        squares = rows[:, :width] * rows[:, :width]
        last = lax.broadcasted_iota(jnp.int32, squares.shape, 1) == width - 1
        density = jnp.sum(jnp.where(last, squares, 0.0), keepdims=True) / count
        high = density.astype(BF16).astype(F32)
        middle = (density - high).astype(BF16).astype(F32)
        low = density - high - middle
        row_index = lax.broadcasted_iota(jnp.int32, (EXTRA, width), 0)
        tail = jnp.where(row_index == 0, high, jnp.where(row_index == 1, middle, low)).astype(BF16)
        for slot in range(slots):
            out_ref[slot, :rows_out, :] = packed
            out_ref[slot, rows_out:, :] = tail

    vmem = pl.BlockSpec(memory_space=pltpu.VMEM)
    operands = [*pieces, *tables, *state]
    shapes = [jax.ShapeDtypeStruct((slots, rows_out + EXTRA, width), BF16)]
    if keeps:
        shapes.append(jax.ShapeDtypeStruct((2 * count, 2 * width), F32))
    return pl.pallas_call(
        body,
        out_shape=tuple(shapes),
        in_specs=[vmem] * len(operands),
        out_specs=tuple([vmem] * len(shapes)),
        scratch_shapes=[pltpu.VMEM((2 * count, 2 * width), F32)],
        compiler_params=pltpu.CompilerParams(vmem_limit_bytes=8 * MIB),
        name="self_energy",
    )(*operands)


def turn(values):
    return [values[1], -values[0], values[3], -values[2]]


def rotate(values, phases):
    cos_part = jnp.cos(phases)
    sin_part = jnp.sin(phases)
    return [
        cos_part * values[0] + sin_part * values[1],
        cos_part * values[1] - sin_part * values[0],
        cos_part * values[2] + sin_part * values[3],
        cos_part * values[3] - sin_part * values[2],
    ]


def advance(received, history, moms, wave, final=None):
    slots, _, width = received.shape
    rows = slots * width
    span = 4 * moms

    def body(*refs):
        recv_ref, less_ref, great_ref, diag_ref, *refs, lhs_ref = refs
        tm_pos = lax.axis_index("tm")
        for slot in range(slots):
            block = recv_ref[slot, :span, :]
            low = jnp.where(slot <= tm_pos, 1.0, 0.0).astype(BF16)
            upp = jnp.where(slot > tm_pos, 1.0, 0.0).astype(BF16)
            cols = pl.ds(slot * width, width)
            lhs_ref[:span, cols] = block * low
            lhs_ref[span:, cols] = block * upp
        own = recv_ref[tm_pos, :span, :]
        lhs = lhs_ref[...]
        row_mom = lax.broadcasted_iota(jnp.int32, (2 * span, 1), 0) % moms
        masks = [jnp.where(row_mom == mom, 1.0, 0.0).astype(BF16) for mom in range(moms)]
        spread = jnp.concatenate([own * mask[:span] for mask in masks], axis=1)
        change = jnp.dot(spread, diag_ref[...], preferred_element_type=F32)
        total = None
        for mom in range(moms):
            main = [less_ref[0, mom], less_ref[1, mom], great_ref[0, mom], great_ref[1, mom]]
            prod = jnp.dot(lhs * masks[mom], jnp.concatenate(main, axis=1), preferred_element_type=F32)
            total = prod if total is None else total + prod

        def product(table, row, col):
            def pick(i, j):
                return table[(row + i) * moms : (row + i + 1) * moms, (col + j) * width : (col + j + 1) * width]

            return pick(0, 0) - pick(1, 1), pick(0, 1) + pick(1, 0)

        low_gl = product(total, 2, 0)
        low_lg = product(total, 0, 2)
        upp_gl = product(total, 6, 0)
        upp_ll = product(total, 4, 0)
        upp_gg = product(total, 6, 2)
        upp_lg = product(total, 4, 2)
        own_less = product(change, 0, 0)
        own_great = product(change, 2, 0)
        memory = [low_gl[i] - low_lg[i] + upp_gl[i] - upp_ll[i] - own_less[i] for i in range(2)]
        memory += [low_gl[i] - low_lg[i] + upp_gg[i] - upp_lg[i] - own_great[i] for i in range(2)]
        tail = recv_ref[slots - 1, 4 * moms :, :].astype(F32)
        density = tail[0:1] + tail[1:2] + tail[2:3]
        mean = density if wave is None else 0.5 * (refs[0][2:3] + density)
        if final is None:
            full_ref, sent_ref, wave_ref = refs[-3:]
            for i in range(4):
                full_ref[i] = memory[i]
                sent_ref[i] = memory[i].astype(BF16)
            phase = (coupling * time_step) * mean
            wave_ref[0:1] = jnp.cos(phase)
            wave_ref[1:2] = jnp.sin(phase)
            wave_ref[2:] = jnp.broadcast_to(density, (6, width))
        else:
            energy_ref, row_ref, kept_ref = refs[1:4]
            mom_pos = lax.axis_index("mom")
            half = 0.5 * time_step
            kept_turn = turn([kept_ref[i] for i in range(4)])
            turned = turn(memory)
            current = []
            for i in range(4):
                start = pl.multiple_of(mom_pos * moms + (i % 2) * (row_ref.shape[0] // 2), moms)
                current.append(row_ref[pl.ds(start, moms), (i // 2) * width : (i // 2 + 1) * width])
            phases = (energy_ref[...] + coupling * mean) * time_step
            trial = rotate([current[i] + half * kept_turn[i] for i in range(4)], phases)
            for i in range(4):
                refs[4 + i // 2][i % 2] = trial[i] + half * turned[i]

    vmem = pl.BlockSpec(memory_space=pltpu.VMEM)
    operands = [received, *history]
    if wave is not None:
        operands.append(wave)
    if final is None:
        block = (4, moms, width)
        shapes = [jax.ShapeDtypeStruct(block, F32), jax.ShapeDtypeStruct(block, BF16)]
        shapes.append(jax.ShapeDtypeStruct((8, width), F32))
    else:
        operands += final
        shapes = [jax.ShapeDtypeStruct((2, moms, width), F32)] * 2
    return pl.pallas_call(
        body,
        out_shape=tuple(shapes),
        in_specs=[vmem] * len(operands),
        out_specs=tuple([vmem] * len(shapes)),
        scratch_shapes=[pltpu.VMEM((2 * span, rows), BF16)],
        compiler_params=pltpu.CompilerParams(vmem_limit_bytes=16 * MIB),
        name="advance",
    )(*operands)


def per_device(hist_less, hist_great, row_less, row_great, mom_table):
    moms, width = row_less.shape[1:]
    mom_count = lax.axis_size("mom")
    time_count = lax.axis_size("tm")
    diagonal, forward, backward, energy, waves = prepare(hist_less, hist_great, mom_table, mom_count)
    history = [
        pltpu.with_memory_space_constraint(hist_less, pltpu.VMEM),
        pltpu.with_memory_space_constraint(hist_great, pltpu.VMEM),
        diagonal,
    ]

    def evaluate(kind, own, sent, state, wave, final=None):
        pieces = [own]
        for step in range(1, mom_count):
            pairs = [(i, i ^ step) for i in range(mom_count)]
            pieces.append(lax.ppermute(sent, "mom", pairs))
        payload, *kept = self_energy(kind, pieces, (forward, backward, waves), state, time_count)
        return kept, advance(lax.all_to_all(payload, "tm", 0, 0), history, moms, wave, final)

    current = jnp.pad(row_less, ((0, 2), (0, 0), (0, 0))) + jnp.pad(row_great, ((2, 0), (0, 0), (0, 0)))
    (row,), (own, sent, wave) = evaluate("start", current, current, (), None)
    for index_new in range(NEW):
        start_own, start_wave = own, wave
        (kept,), (own, sent, wave) = evaluate("predict", own, sent, (row, wave), start_wave)
        for index_pass in range(1, PASS):
            final = (energy, row, start_own) if (index_new, index_pass) == (NEW - 1, PASS - 1) else None
            _, made = evaluate("correct", own, sent, (row, kept, wave), start_wave, final)
            if final is None:
                own, sent, wave = made
        if index_new + 1 < NEW:
            (row,), (own, sent, wave) = evaluate("finish", own, sent, (row, kept, wave), None)
    return made


def solution(mesh):
    return jax.shard_map(
        per_device,
        mesh=mesh,
        in_specs=(
            P(None, "mom", None, "tm"),
            P(None, "mom", None, "tm"),
            P(None, "mom", "tm"),
            P(None, "mom", "tm"),
            P(),
        ),
        out_specs=(P(None, "mom", "tm"), P(None, "mom", "tm")),
        check_vma=False,
    )
```
